128 devices in a mesh: src: 16 (over x_lo, z, core), tgt: 8 (over y, x_hi).
Axes of the slice: x: 4 (x_hi: 2, x_lo: 2; x = x_hi * 2 + x_lo), y: 4, z: 4, core: 2. Of those that a mesh axis runs over, the one named last changes fastest.
Arguments:
- source_field: bfloat16 [1024, 1024, 256], P(None, ('src', 'tgt')), may hold values from -6 to 6
- self_weight: bfloat16 [4, 1024, 256, 256], P(None, ('src', 'tgt')), may hold values from -0.25 to 0.25
- cross_weight: bfloat16 [4, 1024, 256, 256], P(None, ('src', 'tgt')), may hold values from -0.25 to 0.25
- level_bias: float32 [4, 1024, 256], P(None, ('src', 'tgt')), may hold values from -3 to 3
- switch_weight: bfloat16 [1024, 256, 256], P(('src', 'tgt')), may hold values from -0.375 to 0.375
- switch_bias: float32 [1024, 256], P(('src', 'tgt')), may hold values from -3 to 3
Outputs:
- target_field: bfloat16 [1024, 1024, 256], P(None, ('src', 'tgt'))
The draws below stay inside these ranges and needn't reach their ends.
All inputs are finite; a program needn't handle non-finite values.
Results may differ from the reference program's by a relative error of at most 0.0057.
Values may be sent and summed in bfloat16 or wider, within the bound.
A program may use at most 64 MiB of HBM per device.

```python
import jax
import jax.numpy as jnp
from jax import lax

W = 256
BLK_DEV = 8
SHOTS = 1024
LEVELS = 4
NB = 1024
STRIDE = 64
GROUP = 8
PIECE = 32


def level_of(stream_key, shape, shards, least, high):
    level, own = 1.0, jax.random.fold_in(stream_key, 6)
    for dim, shards_of in shards:
        heights = jnp.exp(jax.random.uniform(jax.random.fold_in(own, dim), (shards_of,), jnp.float32, least / len(shards), high / len(shards)))
        level = level * jnp.repeat(heights, shape[dim] // shards_of).reshape([-1 if axis == dim else 1 for axis in range(len(shape))])
    return level


def noise(rng, dims, spread, limit, shards=(), dtype=jnp.bfloat16):
    entries = spread * jax.random.normal(rng, dims, jnp.float32)
    if shards:
        entries = entries * level_of(rng, dims, shards, -0.22, 0.18)
    return jnp.clip(entries, -limit, limit).astype(dtype)


def setup_inputs(seed: int = 0) -> dict:
    splits = jax.random.split(jax.random.key(seed), 7)
    source_field = noise(splits[0], (SHOTS, NB, W), 1.0, 6.0, ((1, 128),))
    self_weight = noise(splits[1], (LEVELS, NB, W, W), (2 * W) ** -0.5, 0.25, ((1, 128),))
    cross_weight = noise(splits[2], (LEVELS, NB, W, W), (2 * W) ** -0.5, 0.25, ((1, 128),))
    level_bias = noise(splits[3], (LEVELS, NB, W), 0.5, 3.0, ((1, 128),), jnp.float32)
    switch_weight = noise(splits[4], (NB, W, W), W ** -0.5, 0.375, ((0, 128),))
    switch_bias = noise(splits[5], (NB, W), 0.5, 3.0, ((0, 128),), jnp.float32)
    return dict(source_field=source_field, self_weight=self_weight, cross_weight=cross_weight, level_bias=level_bias, switch_weight=switch_weight, switch_bias=switch_bias)


def partner(values, dist):
    shots, blocks, width = values.shape
    grouped = values.reshape(shots, blocks // (2 * dist), 2, dist, width)
    return grouped[:, :, ::-1].reshape(shots, blocks, width)


def level_step(field, self_w, cross_w, bias, dist):
    inputs = field.astype(jnp.float32)
    own_part = jnp.einsum("sbi,bio->sbo", inputs, self_w.astype(jnp.float32), precision=lax.Precision.HIGHEST)
    term = jnp.einsum("sbi,bio->sbo", inputs, cross_w.astype(jnp.float32), precision=lax.Precision.HIGHEST)
    term = lax.optimization_barrier(term.astype(jnp.bfloat16))
    moved = partner(term, dist).astype(jnp.float32)
    return jax.nn.relu(own_part + moved + bias[None]).astype(jnp.bfloat16)


def reference(source_field, self_weight, cross_weight, level_bias, switch_weight, switch_bias):
    distances = [STRIDE, NB // 2, NB // 4, 2 * STRIDE]
    field = source_field
    for layer_index in range(2):
        field = level_step(field, self_weight[layer_index], cross_weight[layer_index], level_bias[layer_index], distances[layer_index])
    shaped = field.reshape(SHOTS, NB // (GROUP * BLK_DEV), GROUP, BLK_DEV, GROUP, PIECE)
    mixed = jnp.transpose(shaped, (0, 1, 4, 3, 2, 5)).reshape(SHOTS, NB, W)
    product = jnp.einsum("sbi,bio->sbo", mixed.astype(jnp.float32), switch_weight.astype(jnp.float32), precision=lax.Precision.HIGHEST)
    field = jax.nn.relu(product + switch_bias[None]).astype(jnp.bfloat16)
    for layer_index in range(2, 4):
        field = level_step(field, self_weight[layer_index], cross_weight[layer_index], level_bias[layer_index], distances[layer_index])
    return field
```

```python
import functools

import jax
import jax.numpy as jnp
from jax import lax
from jax.experimental import pallas as pl
from jax.experimental.pallas import tpu as pltpu
from jax.sharding import PartitionSpec as P

MESH = pl.DeviceIdType.MESH
BF = jnp.bfloat16
F32 = jnp.float32
CHUNKS = 8
GROUP_ROWS = 256


def mm(a, b):
    return jnp.dot(a, b, preferred_element_type=F32)


def finish(v):
    return jnp.maximum(v, 0.0).astype(BF)


def quarters(tiles):
    return [
        jnp.concatenate([tile[:, 32 * j : 32 * j + 32] for tile in tiles], axis=1)
        for j in range(4)
    ]


def ring(v):
    return lax.rem(v + 8, 4)


def kernel(
    chunks, rows,
    x_hbm, sw_hbm, cw_hbm, lb, gw_hbm, gb, o_hbm,
    xio, xh, ts, tr, hb, h2, ab, mx, zb, h3, rb,
    w1s, w1c, w2s, w2c, ws, wzs, wzc, b2, bz, pin, pout,
    xin_sem, xout_sem, local_sem, w_send, w_recv,
    t_send, t_recv, h_send, h_recv, a_send, a_recv, z_send, z_recv, r_send, r_recv,
):
    s, t = lax.axis_index("src"), lax.axis_index("tgt")
    core, z, x_lo = lax.rem(s, 2), lax.rem(s // 2, 4), s // 8
    x_hi, y = lax.rem(t, 2), t // 2
    x = x_hi * 2 + x_lo

    def dev(x_, y_, z_, core_):
        return ((lax.rem(x_, 2) * 4 + z_) * 2 + core_, y_ * 2 + x_ // 2)

    core_peer = dev(x, y, z, 1 - core)
    x_peer = dev(x_hi * 2 + 1 - x_lo, y, z, core)

    def z_peer(k):
        return dev(x, y, ring(z + k), core)

    def xy_peer(w):
        return dev(ring(x + w // 4), ring(y + lax.rem(w, 4)), z, core)

    span = rows * 8

    def x_copy(c):
        part = pl.ds(pl.multiple_of(c * span, span), span)
        return pltpu.make_async_copy(x_hbm.at[part], xio.at[c], xin_sem.at[c])

    def o_copy(c):
        part = pl.ds(pl.multiple_of(c * span, span), span)
        return pltpu.make_async_copy(xio.at[c], o_hbm.at[part], xout_sem.at[c])

    local = [
        pltpu.make_async_copy(cw_hbm.at[0], w1c, local_sem.at[0]),
        pltpu.make_async_copy(sw_hbm.at[0], w1s, local_sem.at[1]),
        pltpu.make_async_copy(sw_hbm.at[1, pl.ds(4 * x_lo, 4)], w2s.at[pl.ds(0, 4)], local_sem.at[2]),
        pltpu.make_async_copy(cw_hbm.at[1, pl.ds(4 * x_lo, 4)], w2c.at[pl.ds(0, 4)], local_sem.at[3]),
        pltpu.make_async_copy(gw_hbm, ws, local_sem.at[4]),
        pltpu.make_async_copy(sw_hbm.at[pl.ds(2, 2), pl.ds(2 * z, 2)], wzs.at[0], local_sem.at[5]),
        pltpu.make_async_copy(cw_hbm.at[pl.ds(2, 2), pl.ds(2 * z, 2)], wzc.at[0], local_sem.at[6]),
    ]
    x_copy(0).start()
    for copy in local[:2]:
        copy.start()

    barrier = pltpu.get_barrier_semaphore()

    def greet(device):
        pl.semaphore_signal(barrier, inc=1, device_id=device, device_id_type=MESH)

    greet(core_peer)
    for w in range(1, 16):
        greet(xy_peer(w))
    for k in range(1, 4):
        greet(z_peer(k))

    row = lax.broadcasted_iota(jnp.int32, (GROUP_ROWS, GROUP_ROWS), 0)
    col = lax.broadcasted_iota(jnp.int32, (GROUP_ROWS, GROUP_ROWS), 1)
    pin[...] = jnp.where(col == lax.rem(row, 32) * 8 + row // 32, 1.0, 0.0).astype(BF)
    pout[...] = jnp.where(row == lax.rem(col, 32) * 8 + col // 32, 1.0, 0.0).astype(BF)
    bz[0] = lb[pl.ds(2, 2)]

    pl.semaphore_wait(barrier, 19)

    def send(src, dst, send_sem, recv_sem, device):
        pltpu.make_async_remote_copy(
            src_ref=src, dst_ref=dst, send_sem=send_sem, recv_sem=recv_sem,
            device_id=device, device_id_type=MESH,
        ).start()

    def settle(ref, sem):
        pltpu.make_async_copy(ref, ref, sem).wait()

    away = pl.ds(4 * (1 - x_lo), 4)
    send(sw_hbm.at[1, away], w2s.at[pl.ds(4, 4)], w_send.at[0], w_recv.at[0], x_peer)
    send(cw_hbm.at[1, away], w2c.at[pl.ds(4, 4)], w_send.at[1], w_recv.at[1], x_peer)
    send(lb.at[1], b2, w_send.at[2], w_recv.at[2], x_peer)
    for k in range(1, 4):
        blocks = pl.ds(2 * ring(z + k), 2)
        send(sw_hbm.at[pl.ds(2, 2), blocks], wzs.at[k], w_send.at[3], w_recv.at[3], z_peer(k))
        send(cw_hbm.at[pl.ds(2, 2), blocks], wzc.at[k], w_send.at[4], w_recv.at[4], z_peer(k))
        send(lb.at[pl.ds(2, 2)], bz.at[k], w_send.at[5], w_recv.at[5], z_peer(k))
    for copy in local[2:]:
        copy.start()

    @pl.loop(1, chunks)
    def _(c):
        x_copy(c).start()

    local[0].wait()

    def term_stage(c):
        x_copy(c).wait()

        @pl.loop(0, rows // 32)
        def _(g):
            part = pl.ds(pl.multiple_of(g * GROUP_ROWS, GROUP_ROWS), GROUP_ROWS)
            v = mm(pin[...], xio[c, part]).astype(BF)
            dst = pl.ds(pl.multiple_of(g * 32, 32), 32)
            for l in range(8):
                xh[c, l, dst] = v[32 * l : 32 * l + 32]

        @pl.loop(0, 8)
        def _(l):
            ts[c, l] = mm(xh[c, l], w1c[l]).astype(BF)

        send(ts.at[c], tr.at[c], t_send, t_recv.at[c], core_peer)

    def first_stage(c):
        settle(tr.at[c], t_recv.at[c])

        @pl.loop(0, 8)
        def _(l):
            v = mm(xh[c, l], w1s[l]) + tr[c, l].astype(F32) + lb[0, pl.ds(l, 1)]
            hb[c, l] = finish(v)

        send(hb.at[c, away], hb.at[c, pl.ds(8, 4)], h_send, h_recv.at[c], x_peer)

    def second_stage(c):
        settle(hb.at[c, pl.ds(8, 4)], h_recv.at[c])

        @pl.loop(0, 4)
        def _(m):
            l = 4 * x_lo + m
            mine, other = hb[c, l], hb[c, 8 + m]
            h2[m] = finish(mm(mine, w2s[m]) + mm(other, w2c[4 + m]) + lb[1, pl.ds(l, 1)])
            h2[4 + m] = finish(mm(other, w2s[4 + m]) + mm(mine, w2c[m]) + b2[pl.ds(l, 1)])

        @pl.loop(0, 2)
        def _(side):
            x_to = x_lo + side - 2 * x_lo * side
            for half in range(2):
                lanes = pl.ds(128 * half, 128)
                out = quarters([h2[4 * side + m, :, lanes] for m in range(4)])
                for u in range(4):
                    j = 4 * half + u
                    r = ring((j % 2) * 2 + x_to - x)
                    q = ring(j // 2 - y)
                    ab[c, r * 4 + q] = out[u]

        for w in range(1, 16):
            send(ab.at[c, w], ab.at[c, 15 + w], a_send, a_recv.at[c], xy_peer(w))

    def switch_stage(c):
        settle(ab.at[c, pl.ds(16, 15)], a_recv.at[c])

        @pl.loop(0, 2)
        def _(e):
            for half in range(2):
                tiles = []
                for u in range(4):
                    g = 4 * half + u
                    r = ring(x - ((g % 2) * 2 + e))
                    q = ring(y - g // 2)
                    w = r * 4 + q
                    tiles.append(ab[c, w + 15 * jnp.minimum(w, 1)])
                out = quarters(tiles)
                for m in range(4):
                    mx[4 * e + m, :, pl.ds(128 * half, 128)] = out[m]

        @pl.loop(0, 8)
        def _(l):
            v = mm(mx[l], ws[l]) + gb[pl.ds(l, 1)]
            zb[c, ring(l // 2 - z), lax.rem(l, 2)] = finish(v)

        for k in range(1, 4):
            send(zb.at[c, k], zb.at[c, 3 + k], z_send, z_recv.at[c], z_peer(k))

    def last_stage(c):
        settle(zb.at[c, pl.ds(4, 3)], z_recv.at[c])

        @pl.loop(0, 2)
        def _(n):
            bias = pl.ds(2 * z + n, 1)

            @pl.loop(0, 4)
            def _(k):
                k2 = lax.rem(k + 2, 4)
                a = zb[c, k + 3 * jnp.minimum(k, 1), n]
                b = zb[c, k2 + 3 * jnp.minimum(k2, 1), n]
                h3[k] = finish(mm(a, wzs[k, 0, n]) + mm(b, wzc[k2, 0, n]) + bz[k, 0, bias])

            @pl.loop(0, 4)
            def _(k):
                home = ring(z - k)
                k1 = ring(z - (home + 1 - 2 * lax.rem(home, 2)))
                v = mm(h3[k], wzs[k, 1, n]) + mm(h3[k1], wzc[k1, 1, n]) + bz[k, 1, bias]
                rb[c, k, n] = finish(v)

        for k in range(1, 4):
            send(rb.at[c, k], rb.at[c, 3 + k], r_send, r_recv.at[c], z_peer(4 - k))

    def output_stage(c):
        settle(rb.at[c, pl.ds(4, 3)], r_recv.at[c])

        @pl.loop(0, rows // 32)
        def _(g):
            src = pl.ds(pl.multiple_of(g * 32, 32), 32)
            parts = []
            for l in range(8):
                k = ring(l // 2 - z)
                parts.append(rb[c, k + 3 * jnp.minimum(k, 1), l % 2, src])
            v = mm(pout[...], jnp.concatenate(parts, axis=0)).astype(BF)
            xio[c, pl.ds(pl.multiple_of(g * GROUP_ROWS, GROUP_ROWS), GROUP_ROWS)] = v

        o_copy(c).start()

    term_stage(0)
    local[1].wait()

    @pl.loop(0, chunks + 4)
    def _(step):
        @pl.when(step + 1 < chunks)
        def _():
            term_stage(step + 1)

        @pl.when(step < chunks)
        def _():
            first_stage(step)

        @pl.when(step == 1)
        def _():
            for copy in local[2:5]:
                copy.wait()
            settle(w2s.at[pl.ds(4, 4)], w_recv.at[0])
            settle(w2c.at[pl.ds(4, 4)], w_recv.at[1])
            settle(b2, w_recv.at[2])

        @pl.when((step >= 1) & (step <= chunks))
        def _():
            second_stage(step - 1)

        @pl.when((step >= 2) & (step <= chunks + 1))
        def _():
            switch_stage(step - 2)

        @pl.when(step == 3)
        def _():
            for copy in local[5:]:
                copy.wait()
            settle(wzs.at[pl.ds(1, 3)], w_recv.at[3])
            settle(wzc.at[pl.ds(1, 3)], w_recv.at[4])
            settle(bz.at[pl.ds(1, 3)], w_recv.at[5])

        @pl.when((step >= 3) & (step <= chunks + 2))
        def _():
            last_stage(step - 3)

        @pl.when(step >= 4)
        def _():
            output_stage(step - 4)

    settle(w2s.at[pl.ds(4, 4)], w_send.at[0])
    settle(w2c.at[pl.ds(4, 4)], w_send.at[1])
    settle(b2, w_send.at[2])
    settle(wzs.at[pl.ds(1, 3)], w_send.at[3])
    settle(wzc.at[pl.ds(1, 3)], w_send.at[4])
    settle(bz.at[pl.ds(1, 3)], w_send.at[5])

    @pl.loop(0, chunks)
    def _(c):
        settle(ts.at[c], t_send)
        settle(hb.at[c, pl.ds(8, 4)], h_send)
        settle(ab.at[c, pl.ds(16, 15)], a_send)
        settle(zb.at[c, pl.ds(4, 3)], z_send)
        settle(rb.at[c, pl.ds(4, 3)], r_send)
        o_copy(c).wait()


def per_device(source_field, self_weight, cross_weight, level_bias, switch_weight, switch_bias):
    shots, blocks, width = source_field.shape
    chunks = CHUNKS
    rows = shots // chunks
    anywhere = pl.BlockSpec(memory_space=pl.ANY)
    vmem = pl.BlockSpec(memory_space=pltpu.VMEM)
    dma = pltpu.SemaphoreType.DMA
    square = (width, width)
    out = pl.pallas_call(
        functools.partial(kernel, chunks, rows),
        out_shape=jax.ShapeDtypeStruct((shots * blocks, width), BF),
        in_specs=[anywhere, anywhere, anywhere, vmem, anywhere, vmem],
        out_specs=anywhere,
        scratch_shapes=[
            pltpu.VMEM((chunks, rows * 8, width), BF),
            pltpu.VMEM((chunks, 8, rows, width), BF),
            pltpu.VMEM((chunks, 8, rows, width), BF),
            pltpu.VMEM((chunks, 8, rows, width), BF),
            pltpu.VMEM((chunks, 12, rows, width), BF),
            pltpu.VMEM((8, rows, width), BF),
            pltpu.VMEM((chunks, 31, rows, 128), BF),
            pltpu.VMEM((8, rows, width), BF),
            pltpu.VMEM((chunks, 7, 2, rows, width), BF),
            pltpu.VMEM((4, rows, width), BF),
            pltpu.VMEM((chunks, 7, 2, rows, width), BF),
            pltpu.VMEM((8,) + square, BF),
            pltpu.VMEM((8,) + square, BF),
            pltpu.VMEM((8,) + square, BF),
            pltpu.VMEM((8,) + square, BF),
            pltpu.VMEM((8,) + square, BF),
            pltpu.VMEM((4, 2, 2) + square, BF),
            pltpu.VMEM((4, 2, 2) + square, BF),
            pltpu.VMEM((8, width), F32),
            pltpu.VMEM((4, 2, 8, width), F32),
            pltpu.VMEM((GROUP_ROWS, GROUP_ROWS), BF),
            pltpu.VMEM((GROUP_ROWS, GROUP_ROWS), BF),
            dma((chunks,)), dma((chunks,)), dma((7,)), dma((6,)), dma((6,)),
            dma, dma((chunks,)),
            dma, dma((chunks,)),
            dma, dma((chunks,)),
            dma, dma((chunks,)),
            dma, dma((chunks,)),
        ],
        compiler_params=pltpu.CompilerParams(
            collective_id=0, has_side_effects=True, vmem_limit_bytes=64 * 1024 * 1024 - 65536
        ),
        name="butterfly",
    )(
        source_field.reshape(shots * blocks, width),
        self_weight, cross_weight, level_bias, switch_weight, switch_bias,
    )
    return out.reshape(shots, blocks, width)


def solution(mesh):
    placed = (
        P(None, ("src", "tgt"), None),
        P(None, ("src", "tgt"), None, None),
        P(None, ("src", "tgt"), None, None),
        P(None, ("src", "tgt"), None),
        P(("src", "tgt"), None, None),
        P(("src", "tgt"), None),
    )
    return jax.shard_map(
        per_device,
        mesh=mesh,
        in_specs=placed,
        out_specs=P(None, ("src", "tgt"), None),
        check_vma=False,
    )
```

```python
import functools

import jax
import jax.numpy as jnp
from jax import lax
from jax.experimental import pallas as pl
from jax.experimental.pallas import tpu as pltpu
from jax.sharding import PartitionSpec as P

MESH = pl.DeviceIdType.MESH
BF = jnp.bfloat16
F32 = jnp.float32
CHUNKS = 8
GROUP_ROWS = 256


def mm(a, b):
    return jnp.dot(a, b, preferred_element_type=F32)


def finish(v):
    return jnp.maximum(v, 0.0).astype(BF)


def quarters(tiles):
    return [
        jnp.concatenate([tile[:, 32 * j : 32 * j + 32] for tile in tiles], axis=1)
        for j in range(4)
    ]


def ring(v):
    return lax.rem(v + 8, 4)


def kernel(
    chunks, rows,
    x_hbm, sw_hbm, cw_hbm, lb, gw_hbm, gb, o_hbm,
    xio, xh, ts, tr, hb, h2, ab, mx, zb, h3, rb,
    w1s, w1c, w2s, w2c, ws, wzs, wzc, b2, bz, pin, pout,
    xin_sem, xout_sem, local_sem, w_send, w_recv,
    t_send, t_recv, h_send, h_recv, a_send, a_recv, z_send, z_recv, r_send, r_recv,
):
    s, t = lax.axis_index("src"), lax.axis_index("tgt")
    core, z, x_lo = lax.rem(s, 2), lax.rem(s // 2, 4), s // 8
    x_hi, y = lax.rem(t, 2), t // 2
    x = x_hi * 2 + x_lo

    def dev(x_, y_, z_, core_):
        return ((lax.rem(x_, 2) * 4 + z_) * 2 + core_, y_ * 2 + x_ // 2)

    core_peer = dev(x, y, z, 1 - core)
    x_peer = dev(x_hi * 2 + 1 - x_lo, y, z, core)

    def z_peer(k):
        return dev(x, y, ring(z + k), core)

    def xy_peer(w):
        return dev(ring(x + w // 4), ring(y + lax.rem(w, 4)), z, core)

    span = rows * 8

    def x_copy(c):
        part = pl.ds(pl.multiple_of(c * span, span), span)
        return pltpu.make_async_copy(x_hbm.at[part], xio.at[c], xin_sem.at[c])

    def o_copy(c):
        part = pl.ds(pl.multiple_of(c * span, span), span)
        return pltpu.make_async_copy(xio.at[c], o_hbm.at[part], xout_sem.at[c])

    local = [
        pltpu.make_async_copy(cw_hbm.at[0], w1c, local_sem.at[0]),
        pltpu.make_async_copy(sw_hbm.at[0], w1s, local_sem.at[1]),
        pltpu.make_async_copy(sw_hbm.at[1, pl.ds(4 * x_lo, 4)], w2s.at[pl.ds(0, 4)], local_sem.at[2]),
        pltpu.make_async_copy(cw_hbm.at[1, pl.ds(4 * x_lo, 4)], w2c.at[pl.ds(0, 4)], local_sem.at[3]),
        pltpu.make_async_copy(gw_hbm, ws, local_sem.at[4]),
        pltpu.make_async_copy(sw_hbm.at[pl.ds(2, 2), pl.ds(2 * z, 2)], wzs.at[0], local_sem.at[5]),
        pltpu.make_async_copy(cw_hbm.at[pl.ds(2, 2), pl.ds(2 * z, 2)], wzc.at[0], local_sem.at[6]),
    ]
    x_copy(0).start()
    for copy in local[:2]:
        copy.start()

    barrier = pltpu.get_barrier_semaphore()

    def greet(device):
        pl.semaphore_signal(barrier, inc=1, device_id=device, device_id_type=MESH)

    greet(core_peer)
    for w in range(1, 16):
        greet(xy_peer(w))
    for k in range(1, 4):
        greet(z_peer(k))

    row = lax.broadcasted_iota(jnp.int32, (GROUP_ROWS, GROUP_ROWS), 0)
    col = lax.broadcasted_iota(jnp.int32, (GROUP_ROWS, GROUP_ROWS), 1)
    pin[...] = jnp.where(col == lax.rem(row, 32) * 8 + row // 32, 1.0, 0.0).astype(BF)
    pout[...] = jnp.where(row == lax.rem(col, 32) * 8 + col // 32, 1.0, 0.0).astype(BF)
    bz[0] = lb[pl.ds(2, 2)]

    pl.semaphore_wait(barrier, 19)

    def send(src, dst, send_sem, recv_sem, device):
        pltpu.make_async_remote_copy(
            src_ref=src, dst_ref=dst, send_sem=send_sem, recv_sem=recv_sem,
            device_id=device, device_id_type=MESH,
        ).start()

    def settle(ref, sem):
        pltpu.make_async_copy(ref, ref, sem).wait()

    away = pl.ds(4 * (1 - x_lo), 4)
    send(sw_hbm.at[1, away], w2s.at[pl.ds(4, 4)], w_send.at[0], w_recv.at[0], x_peer)
    send(cw_hbm.at[1, away], w2c.at[pl.ds(4, 4)], w_send.at[1], w_recv.at[1], x_peer)
    send(lb.at[1], b2, w_send.at[2], w_recv.at[2], x_peer)
    for k in range(1, 4):
        blocks = pl.ds(2 * ring(z + k), 2)
        send(sw_hbm.at[pl.ds(2, 2), blocks], wzs.at[k], w_send.at[3], w_recv.at[3], z_peer(k))
        send(cw_hbm.at[pl.ds(2, 2), blocks], wzc.at[k], w_send.at[4], w_recv.at[4], z_peer(k))
        send(lb.at[pl.ds(2, 2)], bz.at[k], w_send.at[5], w_recv.at[5], z_peer(k))
    for copy in local[2:]:
        copy.start()

    @pl.loop(1, chunks)
    def _(c):
        x_copy(c).start()

    local[0].wait()

    def term_stage(c):
        x_copy(c).wait()

        for g in range(rows // 32):
            part = pl.ds(pl.multiple_of(g * GROUP_ROWS, GROUP_ROWS), GROUP_ROWS)
            v = mm(pin[...], xio[c, part]).astype(BF)
            dst = pl.ds(pl.multiple_of(g * 32, 32), 32)
            for l in range(8):
                xh[c, l, dst] = v[32 * l : 32 * l + 32]

        for l in range(8):
            ts[c, l] = mm(xh[c, l], w1c[l]).astype(BF)

        send(ts.at[c], tr.at[c], t_send, t_recv.at[c], core_peer)

    def first_stage(c):
        settle(tr.at[c], t_recv.at[c])

        for l in range(8):
            v = mm(xh[c, l], w1s[l]) + tr[c, l].astype(F32) + lb[0, pl.ds(l, 1)]
            hb[c, l] = finish(v)

        send(hb.at[c, away], hb.at[c, pl.ds(8, 4)], h_send, h_recv.at[c], x_peer)

    def second_stage(c):
        settle(hb.at[c, pl.ds(8, 4)], h_recv.at[c])

        for m in range(4):
            l = 4 * x_lo + m
            mine, other = hb[c, l], hb[c, 8 + m]
            h2[m] = finish(mm(mine, w2s[m]) + mm(other, w2c[4 + m]) + lb[1, pl.ds(l, 1)])
            h2[4 + m] = finish(mm(other, w2s[4 + m]) + mm(mine, w2c[m]) + b2[pl.ds(l, 1)])

        for side in range(2):
            x_to = x_lo + side - 2 * x_lo * side
            for half in range(2):
                lanes = pl.ds(128 * half, 128)
                out = quarters([h2[4 * side + m, :, lanes] for m in range(4)])
                for u in range(4):
                    j = 4 * half + u
                    r = ring((j % 2) * 2 + x_to - x)
                    q = ring(j // 2 - y)
                    ab[c, r * 4 + q] = out[u]

        for w in range(1, 16):
            send(ab.at[c, w], ab.at[c, 15 + w], a_send, a_recv.at[c], xy_peer(w))

    def switch_stage(c):
        settle(ab.at[c, pl.ds(16, 15)], a_recv.at[c])

        for e in range(2):
            for half in range(2):
                tiles = []
                for u in range(4):
                    g = 4 * half + u
                    r = ring(x - ((g % 2) * 2 + e))
                    q = ring(y - g // 2)
                    w = r * 4 + q
                    tiles.append(ab[c, w + 15 * jnp.minimum(w, 1)])
                out = quarters(tiles)
                for m in range(4):
                    mx[4 * e + m, :, pl.ds(128 * half, 128)] = out[m]

        for l in range(8):
            v = mm(mx[l], ws[l]) + gb[pl.ds(l, 1)]
            zb[c, ring(l // 2 - z), lax.rem(l, 2)] = finish(v)

        for k in range(1, 4):
            send(zb.at[c, k], zb.at[c, 3 + k], z_send, z_recv.at[c], z_peer(k))

    def last_stage(c):
        settle(zb.at[c, pl.ds(4, 3)], z_recv.at[c])

        for n in range(2):
            bias = pl.ds(2 * z + n, 1)

            for k in range(4):
                k2 = lax.rem(k + 2, 4)
                a = zb[c, k + 3 * jnp.minimum(k, 1), n]
                b = zb[c, k2 + 3 * jnp.minimum(k2, 1), n]
                h3[k] = finish(mm(a, wzs[k, 0, n]) + mm(b, wzc[k2, 0, n]) + bz[k, 0, bias])

            for k in range(4):
                home = ring(z - k)
                k1 = ring(z - (home + 1 - 2 * lax.rem(home, 2)))
                v = mm(h3[k], wzs[k, 1, n]) + mm(h3[k1], wzc[k1, 1, n]) + bz[k, 1, bias]
                rb[c, k, n] = finish(v)

        for k in range(1, 4):
            send(rb.at[c, k], rb.at[c, 3 + k], r_send, r_recv.at[c], z_peer(4 - k))

    def output_stage(c):
        settle(rb.at[c, pl.ds(4, 3)], r_recv.at[c])

        for g in range(rows // 32):
            src = pl.ds(pl.multiple_of(g * 32, 32), 32)
            parts = []
            for l in range(8):
                k = ring(l // 2 - z)
                parts.append(rb[c, k + 3 * jnp.minimum(k, 1), l % 2, src])
            v = mm(pout[...], jnp.concatenate(parts, axis=0)).astype(BF)
            xio[c, pl.ds(pl.multiple_of(g * GROUP_ROWS, GROUP_ROWS), GROUP_ROWS)] = v

        o_copy(c).start()

    term_stage(0)
    local[1].wait()

    @pl.loop(0, chunks + 4)
    def _(step):
        @pl.when(step + 1 < chunks)
        def _():
            term_stage(step + 1)

        @pl.when(step < chunks)
        def _():
            first_stage(step)

        @pl.when(step == 1)
        def _():
            for copy in local[2:5]:
                copy.wait()
            settle(w2s.at[pl.ds(4, 4)], w_recv.at[0])
            settle(w2c.at[pl.ds(4, 4)], w_recv.at[1])
            settle(b2, w_recv.at[2])

        @pl.when((step >= 1) & (step <= chunks))
        def _():
            second_stage(step - 1)

        @pl.when((step >= 2) & (step <= chunks + 1))
        def _():
            switch_stage(step - 2)

        @pl.when(step == 3)
        def _():
            for copy in local[5:]:
                copy.wait()
            settle(wzs.at[pl.ds(1, 3)], w_recv.at[3])
            settle(wzc.at[pl.ds(1, 3)], w_recv.at[4])
            settle(bz.at[pl.ds(1, 3)], w_recv.at[5])

        @pl.when((step >= 3) & (step <= chunks + 2))
        def _():
            last_stage(step - 3)

        @pl.when(step >= 4)
        def _():
            output_stage(step - 4)

    settle(w2s.at[pl.ds(4, 4)], w_send.at[0])
    settle(w2c.at[pl.ds(4, 4)], w_send.at[1])
    settle(b2, w_send.at[2])
    settle(wzs.at[pl.ds(1, 3)], w_send.at[3])
    settle(wzc.at[pl.ds(1, 3)], w_send.at[4])
    settle(bz.at[pl.ds(1, 3)], w_send.at[5])

    @pl.loop(0, chunks)
    def _(c):
        settle(ts.at[c], t_send)
        settle(hb.at[c, pl.ds(8, 4)], h_send)
        settle(ab.at[c, pl.ds(16, 15)], a_send)
        settle(zb.at[c, pl.ds(4, 3)], z_send)
        settle(rb.at[c, pl.ds(4, 3)], r_send)
        o_copy(c).wait()


def per_device(source_field, self_weight, cross_weight, level_bias, switch_weight, switch_bias):
    shots, blocks, width = source_field.shape
    chunks = CHUNKS
    rows = shots // chunks
    anywhere = pl.BlockSpec(memory_space=pl.ANY)
    vmem = pl.BlockSpec(memory_space=pltpu.VMEM)
    dma = pltpu.SemaphoreType.DMA
    square = (width, width)
    out = pl.pallas_call(
        functools.partial(kernel, chunks, rows),
        out_shape=jax.ShapeDtypeStruct((shots * blocks, width), BF),
        in_specs=[anywhere, anywhere, anywhere, vmem, anywhere, vmem],
        out_specs=anywhere,
        scratch_shapes=[
            pltpu.VMEM((chunks, rows * 8, width), BF),
            pltpu.VMEM((chunks, 8, rows, width), BF),
            pltpu.VMEM((chunks, 8, rows, width), BF),
            pltpu.VMEM((chunks, 8, rows, width), BF),
            pltpu.VMEM((chunks, 12, rows, width), BF),
            pltpu.VMEM((8, rows, width), BF),
            pltpu.VMEM((chunks, 31, rows, 128), BF),
            pltpu.VMEM((8, rows, width), BF),
            pltpu.VMEM((chunks, 7, 2, rows, width), BF),
            pltpu.VMEM((4, rows, width), BF),
            pltpu.VMEM((chunks, 7, 2, rows, width), BF),
            pltpu.VMEM((8,) + square, BF),
            pltpu.VMEM((8,) + square, BF),
            pltpu.VMEM((8,) + square, BF),
            pltpu.VMEM((8,) + square, BF),
            pltpu.VMEM((8,) + square, BF),
            pltpu.VMEM((4, 2, 2) + square, BF),
            pltpu.VMEM((4, 2, 2) + square, BF),
            pltpu.VMEM((8, width), F32),
            pltpu.VMEM((4, 2, 8, width), F32),
            pltpu.VMEM((GROUP_ROWS, GROUP_ROWS), BF),
            pltpu.VMEM((GROUP_ROWS, GROUP_ROWS), BF),
            dma((chunks,)), dma((chunks,)), dma((7,)), dma((6,)), dma((6,)),
            dma, dma((chunks,)),
            dma, dma((chunks,)),
            dma, dma((chunks,)),
            dma, dma((chunks,)),
            dma, dma((chunks,)),
        ],
        compiler_params=pltpu.CompilerParams(
            collective_id=0, has_side_effects=True, vmem_limit_bytes=64 * 1024 * 1024 - 65536
        ),
        name="butterfly",
    )(
        source_field.reshape(shots * blocks, width),
        self_weight, cross_weight, level_bias, switch_weight, switch_bias,
    )
    return out.reshape(shots, blocks, width)


def solution(mesh):
    placed = (
        P(None, ("src", "tgt"), None),
        P(None, ("src", "tgt"), None, None),
        P(None, ("src", "tgt"), None, None),
        P(None, ("src", "tgt"), None),
        P(("src", "tgt"), None, None),
        P(("src", "tgt"), None),
    )
    return jax.shard_map(
        per_device,
        mesh=mesh,
        in_specs=placed,
        out_specs=P(None, ("src", "tgt"), None),
        check_vma=False,
    )
```

```python
import functools

import jax
import jax.numpy as jnp
from jax import lax
from jax.experimental import pallas as pl
from jax.experimental.pallas import tpu as pltpu
from jax.sharding import PartitionSpec as P

MESH = pl.DeviceIdType.MESH
BF = jnp.bfloat16
F32 = jnp.float32
CHUNKS = 8
GROUP_ROWS = 256


def mm(a, b):
    return jnp.dot(a, b, preferred_element_type=F32)


def finish(v):
    return jnp.maximum(v, 0.0).astype(BF)


def quarters(tiles):
    return [
        jnp.concatenate([tile[:, 32 * j : 32 * j + 32] for tile in tiles], axis=1)
        for j in range(4)
    ]


def ring(v):
    return lax.rem(v + 8, 4)


def kernel(
    chunks, rows,
    x_hbm, sw_hbm, cw_hbm, lb_hbm, gw_hbm, gb_hbm, out_ref,
    xio, xh, ts, tr, hb, h2, ab, mx, zb, h3, rb,
    w1s, w1c, w2s, w2c, ws, wzs, wzc, lb, gb, b2, bz, pin, pout,
    xin_sem, local_sem, w_send, w_recv,
    t_send, t_recv, h_send, h_recv, a_send, a_recv, z_send, z_recv, r_send, r_recv,
):
    s, t = lax.axis_index("src"), lax.axis_index("tgt")
    core, z, x_lo = lax.rem(s, 2), lax.rem(s // 2, 4), s // 8
    x_hi, y = lax.rem(t, 2), t // 2
    x = x_hi * 2 + x_lo

    def dev(x_, y_, z_, core_):
        return ((lax.rem(x_, 2) * 4 + z_) * 2 + core_, y_ * 2 + x_ // 2)

    core_peer = dev(x, y, z, 1 - core)
    x_peer = dev(x_hi * 2 + 1 - x_lo, y, z, core)

    def z_peer(k):
        return dev(x, y, ring(z + k), core)

    def xy_peer(w):
        return dev(ring(x + w // 4), ring(y + lax.rem(w, 4)), z, core)

    span = rows * 8

    def x_copy(c):
        part = pl.ds(pl.multiple_of(c * span, span), span)
        return pltpu.make_async_copy(x_hbm.at[part], xio.at[c], xin_sem.at[c])

    local = [
        pltpu.make_async_copy(cw_hbm.at[0], w1c, local_sem.at[0]),
        pltpu.make_async_copy(sw_hbm.at[0], w1s, local_sem.at[1]),
        pltpu.make_async_copy(lb_hbm, lb, local_sem.at[7]),
        pltpu.make_async_copy(sw_hbm.at[1, pl.ds(4 * x_lo, 4)], w2s.at[pl.ds(0, 4)], local_sem.at[2]),
        pltpu.make_async_copy(cw_hbm.at[1, pl.ds(4 * x_lo, 4)], w2c.at[pl.ds(0, 4)], local_sem.at[3]),
        pltpu.make_async_copy(gw_hbm, ws, local_sem.at[4]),
        pltpu.make_async_copy(gb_hbm, gb, local_sem.at[8]),
        pltpu.make_async_copy(sw_hbm.at[pl.ds(2, 2), pl.ds(2 * z, 2)], wzs.at[0], local_sem.at[5]),
        pltpu.make_async_copy(cw_hbm.at[pl.ds(2, 2), pl.ds(2 * z, 2)], wzc.at[0], local_sem.at[6]),
        pltpu.make_async_copy(lb_hbm.at[pl.ds(2, 2)], bz.at[0], local_sem.at[9]),
    ]
    x_copy(0).start()
    for copy in local[:3]:
        copy.start()

    barrier = pltpu.get_barrier_semaphore()

    def greet(device):
        pl.semaphore_signal(barrier, inc=1, device_id=device, device_id_type=MESH)

    greet(core_peer)
    for w in range(1, 16):
        greet(xy_peer(w))
    for k in range(1, 4):
        greet(z_peer(k))

    row = lax.broadcasted_iota(jnp.int32, (GROUP_ROWS, GROUP_ROWS), 0)
    col = lax.broadcasted_iota(jnp.int32, (GROUP_ROWS, GROUP_ROWS), 1)
    pin[...] = jnp.where(col == lax.rem(row, 32) * 8 + row // 32, 1.0, 0.0).astype(BF)
    pout[...] = jnp.where(row == lax.rem(col, 32) * 8 + col // 32, 1.0, 0.0).astype(BF)

    pl.semaphore_wait(barrier, 19)

    def send(src, dst, send_sem, recv_sem, device):
        pltpu.make_async_remote_copy(
            src_ref=src, dst_ref=dst, send_sem=send_sem, recv_sem=recv_sem,
            device_id=device, device_id_type=MESH,
        ).start()

    def settle(ref, sem):
        pltpu.make_async_copy(ref, ref, sem).wait()

    away = pl.ds(4 * (1 - x_lo), 4)
    send(sw_hbm.at[1, away], w2s.at[pl.ds(4, 4)], w_send.at[0], w_recv.at[0], x_peer)
    send(cw_hbm.at[1, away], w2c.at[pl.ds(4, 4)], w_send.at[1], w_recv.at[1], x_peer)
    send(lb_hbm.at[1], b2, w_send.at[2], w_recv.at[2], x_peer)
    for k in (1, 3, 2):
        blocks = pl.ds(2 * ring(z + k), 2)
        send(sw_hbm.at[pl.ds(2, 2), blocks], wzs.at[k], w_send.at[3], w_recv.at[3], z_peer(k))
        send(cw_hbm.at[pl.ds(2, 2), blocks], wzc.at[k], w_send.at[4], w_recv.at[4], z_peer(k))
        send(lb_hbm.at[pl.ds(2, 2)], bz.at[k], w_send.at[5], w_recv.at[5], z_peer(k))
    for copy in local[3:]:
        copy.start()

    @pl.loop(1, chunks)
    def _(c):
        x_copy(c).start()

    local[0].wait()

    def term_stage(c):
        x_copy(c).wait()

        for g in range(rows // 32):
            part = pl.ds(pl.multiple_of(g * GROUP_ROWS, GROUP_ROWS), GROUP_ROWS)
            v = mm(pin[...], xio[c, part]).astype(BF)
            dst = pl.ds(pl.multiple_of(g * 32, 32), 32)
            for l in range(8):
                xh[c, l, dst] = v[32 * l : 32 * l + 32]

        for l in range(8):
            ts[c, l] = mm(xh[c, l], w1c[l]).astype(BF)

        send(ts.at[c], tr.at[c], t_send, t_recv.at[c], core_peer)

    def first_stage(c):
        settle(tr.at[c], t_recv.at[c])
        for side in range(2):
            for m in range(4):
                l = 4 * (1 - x_lo if side == 0 else x_lo) + m
                v = mm(xh[c, l], w1s[l]) + tr[c, l].astype(F32) + lb[0, pl.ds(l, 1)]
                hb[c, l] = finish(v)
            if side == 0:
                send(hb.at[c, away], hb.at[c, pl.ds(8, 4)], h_send, h_recv.at[c], x_peer)

    def second_stage(c):
        settle(hb.at[c, pl.ds(8, 4)], h_recv.at[c])

        for m in range(4):
            l = 4 * x_lo + m
            mine, other = hb[c, l], hb[c, 8 + m]
            h2[m] = finish(mm(mine, w2s[m]) + mm(other, w2c[4 + m]) + lb[1, pl.ds(l, 1)])
            h2[4 + m] = finish(mm(other, w2s[4 + m]) + mm(mine, w2c[m]) + b2[pl.ds(l, 1)])

        for side in range(2):
            x_to = x_lo + side - 2 * x_lo * side
            for half in range(2):
                lanes = pl.ds(128 * half, 128)
                out = quarters([h2[4 * side + m, :, lanes] for m in range(4)])
                for u in range(4):
                    j = 4 * half + u
                    r = ring((j % 2) * 2 + x_to - x)
                    q = ring(j // 2 - y)
                    ab[c, r * 4 + q] = out[u]
        for w in range(1, 16):
            send(ab.at[c, w], ab.at[c, 15 + w], a_send, a_recv.at[c], xy_peer(w))

    def switch_stage(c):
        settle(ab.at[c, pl.ds(16, 15)], a_recv.at[c])

        for e in range(2):
            for half in range(2):
                tiles = []
                for u in range(4):
                    g = 4 * half + u
                    r = ring(x - ((g % 2) * 2 + e))
                    q = ring(y - g // 2)
                    w = r * 4 + q
                    tiles.append(ab[c, w + 15 * jnp.minimum(w, 1)])
                out = quarters(tiles)
                for m in range(4):
                    mx[4 * e + m, :, pl.ds(128 * half, 128)] = out[m]

        for n in range(2):
            for k in (1, 3, 2, 0):
                l = 2 * ring(z + k) + n
                zb[c, n, k] = finish(mm(mx[l], ws[l]) + gb[pl.ds(l, 1)])
            for k in (1, 3, 2):
                send(zb.at[c, n, k], zb.at[c, n, 3 + k], z_send, z_recv.at[c, n], z_peer(k))

    def last_stage(c):
        for n in range(2):
            settle(zb.at[c, n, pl.ds(4, 3)], z_recv.at[c, n])
            bias = pl.ds(2 * z + n, 1)
            held = [zb[c, n, k + 3 if k else 0] for k in range(4)]
            for k in range(4):
                k2 = (k + 2) % 4
                v = mm(held[k], wzs[k, 0, n]) + mm(held[k2], wzc[k2, 0, n]) + bz[k, 0, bias]
                h3[n, k] = finish(v)
            for k in (1, 3, 2, 0):
                home = ring(z - k)
                k1 = ring(z - (home + 1 - 2 * lax.rem(home, 2)))
                v = mm(h3[n, k], wzs[k, 1, n]) + mm(h3[n, k1], wzc[k1, 1, n]) + bz[k, 1, bias]
                rb[c, n, k] = finish(v)
            for k in (1, 3, 2):
                send(rb.at[c, n, k], rb.at[c, n, 3 + k], r_send, r_recv.at[c], z_peer(4 - k))

    def output_stage(c):
        settle(rb.at[c, :, pl.ds(4, 3)], r_recv.at[c])

        for g in range(rows // 32):
            src = pl.ds(pl.multiple_of(g * 32, 32), 32)
            parts = []
            for l in range(8):
                k = ring(l // 2 - z)
                parts.append(rb[c, l % 2, k + 3 * jnp.minimum(k, 1), src])
            v = mm(pout[...], jnp.concatenate(parts, axis=0)).astype(BF)
            out_ref[pl.ds(pl.multiple_of(c * span + g * GROUP_ROWS, GROUP_ROWS), GROUP_ROWS)] = v

    term_stage(0)
    for copy in local[1:3]:
        copy.wait()

    @pl.loop(0, chunks + 4)
    def _(step):
        @pl.when(step + 1 < chunks)
        def _():
            term_stage(step + 1)

        @pl.when(step < chunks)
        def _():
            first_stage(step)

        @pl.when(step == 1)
        def _():
            for copy in local[3:7]:
                copy.wait()
            settle(w2s.at[pl.ds(4, 4)], w_recv.at[0])
            settle(w2c.at[pl.ds(4, 4)], w_recv.at[1])
            settle(b2, w_recv.at[2])

        @pl.when((step >= 1) & (step <= chunks))
        def _():
            second_stage(step - 1)

        @pl.when((step >= 2) & (step <= chunks + 1))
        def _():
            switch_stage(step - 2)

        @pl.when(step == 3)
        def _():
            for copy in local[7:]:
                copy.wait()
            settle(wzs.at[pl.ds(1, 3)], w_recv.at[3])
            settle(wzc.at[pl.ds(1, 3)], w_recv.at[4])
            settle(bz.at[pl.ds(1, 3)], w_recv.at[5])

        @pl.when((step >= 3) & (step <= chunks + 2))
        def _():
            last_stage(step - 3)

        @pl.when(step >= 4)
        def _():
            output_stage(step - 4)

    settle(w2s.at[pl.ds(4, 4)], w_send.at[0])
    settle(w2c.at[pl.ds(4, 4)], w_send.at[1])
    settle(b2, w_send.at[2])
    settle(wzs.at[pl.ds(1, 3)], w_send.at[3])
    settle(wzc.at[pl.ds(1, 3)], w_send.at[4])
    settle(bz.at[pl.ds(1, 3)], w_send.at[5])

    @pl.loop(0, chunks)
    def _(c):
        settle(ts.at[c], t_send)
        settle(hb.at[c, pl.ds(8, 4)], h_send)
        settle(ab.at[c, pl.ds(16, 15)], a_send)
        settle(zb.at[c, :, pl.ds(4, 3)], z_send)
        settle(rb.at[c, :, pl.ds(4, 3)], r_send)


def per_device(source_field, self_weight, cross_weight, level_bias, switch_weight, switch_bias):
    shots, blocks, width = source_field.shape
    chunks = CHUNKS
    rows = shots // chunks
    anywhere = pl.BlockSpec(memory_space=pl.ANY)
    vmem = pl.BlockSpec(memory_space=pltpu.VMEM)
    dma = pltpu.SemaphoreType.DMA
    square = (width, width)
    out = pl.pallas_call(
        functools.partial(kernel, chunks, rows),
        out_shape=pltpu.VMEM((shots * blocks, width), BF),
        in_specs=[anywhere] * 6,
        out_specs=vmem,
        scratch_shapes=[
            pltpu.VMEM((chunks, rows * 8, width), BF),
            pltpu.VMEM((chunks, 8, rows, width), BF),
            pltpu.VMEM((chunks, 8, rows, width), BF),
            pltpu.VMEM((chunks, 8, rows, width), BF),
            pltpu.VMEM((chunks, 12, rows, width), BF),
            pltpu.VMEM((8, rows, width), BF),
            pltpu.VMEM((chunks, 31, rows, 128), BF),
            pltpu.VMEM((8, rows, width), BF),
            pltpu.VMEM((chunks, 2, 7, rows, width), BF),
            pltpu.VMEM((2, 4, rows, width), BF),
            pltpu.VMEM((chunks, 2, 7, rows, width), BF),
            pltpu.VMEM((8,) + square, BF),
            pltpu.VMEM((8,) + square, BF),
            pltpu.VMEM((8,) + square, BF),
            pltpu.VMEM((8,) + square, BF),
            pltpu.VMEM((8,) + square, BF),
            pltpu.VMEM((4, 2, 2) + square, BF),
            pltpu.VMEM((4, 2, 2) + square, BF),
            pltpu.VMEM((4, 8, width), F32),
            pltpu.VMEM((8, width), F32),
            pltpu.VMEM((8, width), F32),
            pltpu.VMEM((4, 2, 8, width), F32),
            pltpu.VMEM((GROUP_ROWS, GROUP_ROWS), BF),
            pltpu.VMEM((GROUP_ROWS, GROUP_ROWS), BF),
            dma((chunks,)), dma((10,)), dma((6,)), dma((6,)),
            dma, dma((chunks,)),
            dma, dma((chunks,)),
            dma, dma((chunks,)),
            dma, dma((chunks, 2)),
            dma, dma((chunks,)),
        ],
        compiler_params=pltpu.CompilerParams(
            collective_id=0, has_side_effects=True, vmem_limit_bytes=56 * 1024 * 1024
        ),
        name="butterfly",
    )(
        source_field.reshape(shots * blocks, width),
        self_weight, cross_weight, level_bias, switch_weight, switch_bias,
    )
    return out.reshape(shots, blocks, width)


def solution(mesh):
    placed = (
        P(None, ("src", "tgt"), None),
        P(None, ("src", "tgt"), None, None),
        P(None, ("src", "tgt"), None, None),
        P(None, ("src", "tgt"), None),
        P(("src", "tgt"), None, None),
        P(("src", "tgt"), None),
    )
    return jax.shard_map(
        per_device,
        mesh=mesh,
        in_specs=placed,
        out_specs=P(None, ("src", "tgt"), None),
        check_vma=False,
    )
```

```python
import functools

import jax
import jax.numpy as jnp
from jax import lax
from jax.experimental import pallas as pl
from jax.experimental.pallas import tpu as pltpu
from jax.sharding import PartitionSpec as P

MESH = pl.DeviceIdType.MESH
BF = jnp.bfloat16
F32 = jnp.float32
CHUNKS = 8
GROUP_ROWS = 256


def mm(a, b):
    return jnp.dot(a, b, preferred_element_type=F32)


def finish(v):
    return jnp.maximum(v, 0.0).astype(BF)


def quarters(tiles):
    return [
        jnp.concatenate([tile[:, 32 * j : 32 * j + 32] for tile in tiles], axis=1)
        for j in range(4)
    ]


def ring(v):
    return lax.rem(v + 8, 4)


def kernel(
    chunks, rows,
    x_hbm, sw_hbm, cw_hbm, lb_hbm, gw_hbm, gb_hbm, out_ref,
    xio, xh, ts, tr, hb, h2, ab, mx, zb, h3, rb,
    w1s, w1c, w2s, w2c, ws, wzs, wzc, lb, gb, b2, bz, pin, pout,
    xin_sem, local_sem, w_send, w_recv,
    t_send, t_recv, h_send, h_recv, a_send, a_recv, z_send, z_recv, r_send, r_recv,
):
    s, t = lax.axis_index("src"), lax.axis_index("tgt")
    core, z, x_lo = lax.rem(s, 2), lax.rem(s // 2, 4), s // 8
    x_hi, y = lax.rem(t, 2), t // 2
    x = x_hi * 2 + x_lo

    def dev(x_, y_, z_, core_):
        return ((lax.rem(x_, 2) * 4 + z_) * 2 + core_, y_ * 2 + x_ // 2)

    core_peer = dev(x, y, z, 1 - core)
    x_peer = dev(x_hi * 2 + 1 - x_lo, y, z, core)

    def z_peer(k):
        return dev(x, y, ring(z + k), core)

    def xy_peer(w):
        return dev(ring(x + w // 4), ring(y + lax.rem(w, 4)), z, core)

    span = rows * 8

    def x_copy(c):
        part = pl.ds(pl.multiple_of(c * span, span), span)
        return pltpu.make_async_copy(x_hbm.at[part], xio.at[c], xin_sem.at[c])

    local = [
        pltpu.make_async_copy(cw_hbm.at[0], w1c, local_sem.at[0]),
        pltpu.make_async_copy(sw_hbm.at[0], w1s, local_sem.at[1]),
        pltpu.make_async_copy(lb_hbm, lb, local_sem.at[7]),
        pltpu.make_async_copy(sw_hbm.at[1, pl.ds(4 * x_lo, 4)], w2s.at[pl.ds(0, 4)], local_sem.at[2]),
        pltpu.make_async_copy(cw_hbm.at[1, pl.ds(4 * x_lo, 4)], w2c.at[pl.ds(0, 4)], local_sem.at[3]),
        pltpu.make_async_copy(gw_hbm, ws, local_sem.at[4]),
        pltpu.make_async_copy(gb_hbm, gb, local_sem.at[8]),
        pltpu.make_async_copy(sw_hbm.at[pl.ds(2, 2), pl.ds(2 * z, 2)], wzs.at[0], local_sem.at[5]),
        pltpu.make_async_copy(cw_hbm.at[pl.ds(2, 2), pl.ds(2 * z, 2)], wzc.at[0], local_sem.at[6]),
        pltpu.make_async_copy(lb_hbm.at[pl.ds(2, 2)], bz.at[0], local_sem.at[9]),
    ]
    barrier = pltpu.get_barrier_semaphore()

    def greet(device):
        pl.semaphore_signal(barrier, inc=1, device_id=device, device_id_type=MESH)

    greet(core_peer)
    for w in range(1, 16):
        greet(xy_peer(w))
    for k in range(1, 4):
        greet(z_peer(k))

    x_copy(0).start()
    for copy in local[:3]:
        copy.start()

    pl.semaphore_wait(barrier, 19)

    def send(src, dst, send_sem, recv_sem, device):
        pltpu.make_async_remote_copy(
            src_ref=src, dst_ref=dst, send_sem=send_sem, recv_sem=recv_sem,
            device_id=device, device_id_type=MESH,
        ).start()

    def settle(ref, sem):
        pltpu.make_async_copy(ref, ref, sem).wait()

    away = pl.ds(4 * (1 - x_lo), 4)
    send(sw_hbm.at[1, away], w2s.at[pl.ds(4, 4)], w_send.at[0], w_recv.at[0], x_peer)
    send(cw_hbm.at[1, away], w2c.at[pl.ds(4, 4)], w_send.at[1], w_recv.at[1], x_peer)
    send(lb_hbm.at[1], b2, w_send.at[2], w_recv.at[2], x_peer)
    for k in (1, 3, 2):
        blocks = pl.ds(2 * ring(z + k), 2)
        send(sw_hbm.at[pl.ds(2, 2), blocks], wzs.at[k], w_send.at[3], w_recv.at[3], z_peer(k))
        send(cw_hbm.at[pl.ds(2, 2), blocks], wzc.at[k], w_send.at[4], w_recv.at[4], z_peer(k))
        send(lb_hbm.at[pl.ds(2, 2)], bz.at[k], w_send.at[5], w_recv.at[5], z_peer(k))
    for copy in local[3:]:
        copy.start()

    @pl.loop(1, chunks)
    def _(c):
        x_copy(c).start()

    row = lax.broadcasted_iota(jnp.int32, (GROUP_ROWS, GROUP_ROWS), 0)
    col = lax.broadcasted_iota(jnp.int32, (GROUP_ROWS, GROUP_ROWS), 1)
    pin[...] = jnp.where(col == lax.rem(row, 32) * 8 + row // 32, 1.0, 0.0).astype(BF)
    pout[...] = jnp.where(row == lax.rem(col, 32) * 8 + col // 32, 1.0, 0.0).astype(BF)

    local[0].wait()

    def term_stage(c):
        x_copy(c).wait()

        for g in range(rows // 32):
            part = pl.ds(pl.multiple_of(g * GROUP_ROWS, GROUP_ROWS), GROUP_ROWS)
            v = mm(pin[...], xio[c, part]).astype(BF)
            dst = pl.ds(pl.multiple_of(g * 32, 32), 32)
            for l in range(8):
                xh[c, l, dst] = v[32 * l : 32 * l + 32]

        for l in range(8):
            ts[c, l] = mm(xh[c, l], w1c[l]).astype(BF)

        send(ts.at[c], tr.at[c], t_send, t_recv.at[c], core_peer)

    def first_stage(c):
        settle(tr.at[c], t_recv.at[c])
        for side in range(2):
            for m in range(4):
                l = 4 * (1 - x_lo if side == 0 else x_lo) + m
                v = mm(xh[c, l], w1s[l]) + tr[c, l].astype(F32) + lb[0, pl.ds(l, 1)]
                hb[c, l] = finish(v)
            if side == 0:
                send(hb.at[c, away], hb.at[c, pl.ds(8, 4)], h_send, h_recv.at[c], x_peer)

    def second_stage(c):
        settle(hb.at[c, pl.ds(8, 4)], h_recv.at[c])

        for m in range(4):
            l = 4 * x_lo + m
            mine, other = hb[c, l], hb[c, 8 + m]
            h2[m] = finish(mm(mine, w2s[m]) + mm(other, w2c[4 + m]) + lb[1, pl.ds(l, 1)])
            h2[4 + m] = finish(mm(other, w2s[4 + m]) + mm(mine, w2c[m]) + b2[pl.ds(l, 1)])

        for side in range(2):
            x_to = x_lo + side - 2 * x_lo * side
            for half in range(2):
                lanes = pl.ds(128 * half, 128)
                out = quarters([h2[4 * side + m, :, lanes] for m in range(4)])
                for u in range(4):
                    j = 4 * half + u
                    r = ring((j % 2) * 2 + x_to - x)
                    q = ring(j // 2 - y)
                    ab[c, r * 4 + q] = out[u]
        for w in range(1, 16):
            send(ab.at[c, w], ab.at[c, 15 + w], a_send, a_recv.at[c], xy_peer(w))

    def switch_stage(c):
        settle(ab.at[c, pl.ds(16, 15)], a_recv.at[c])

        for e in range(2):
            for half in range(2):
                tiles = []
                for u in range(4):
                    g = 4 * half + u
                    r = ring(x - ((g % 2) * 2 + e))
                    q = ring(y - g // 2)
                    w = r * 4 + q
                    tiles.append(ab[c, w + 15 * jnp.minimum(w, 1)])
                out = quarters(tiles)
                for m in range(4):
                    mx[4 * e + m, :, pl.ds(128 * half, 128)] = out[m]

        for n in range(2):
            for k in (1, 3, 2, 0):
                l = 2 * ring(z + k) + n
                zb[c, n, k] = finish(mm(mx[l], ws[l]) + gb[pl.ds(l, 1)])
            for k in (1, 3, 2):
                send(zb.at[c, n, k], zb.at[c, n, 3 + k], z_send, z_recv.at[c, n], z_peer(k))

    def last_stage(c):
        for n in range(2):
            settle(zb.at[c, n, pl.ds(4, 3)], z_recv.at[c, n])
            bias = pl.ds(2 * z + n, 1)
            held = [zb[c, n, k + 3 if k else 0] for k in range(4)]
            for k in range(4):
                k2 = (k + 2) % 4
                v = mm(held[k], wzs[k, 0, n]) + mm(held[k2], wzc[k2, 0, n]) + bz[k, 0, bias]
                h3[n, k] = finish(v)
            for k in (1, 3, 2, 0):
                home = ring(z - k)
                k1 = ring(z - (home + 1 - 2 * lax.rem(home, 2)))
                v = mm(h3[n, k], wzs[k, 1, n]) + mm(h3[n, k1], wzc[k1, 1, n]) + bz[k, 1, bias]
                rb[c, n, k] = finish(v)
            for k in (1, 3, 2):
                send(rb.at[c, n, k], rb.at[c, n, 3 + k], r_send, r_recv.at[c], z_peer(4 - k))

    def output_stage(c):
        settle(rb.at[c, :, pl.ds(4, 3)], r_recv.at[c])

        for g in range(rows // 32):
            src = pl.ds(pl.multiple_of(g * 32, 32), 32)
            parts = []
            for l in range(8):
                k = ring(l // 2 - z)
                parts.append(rb[c, l % 2, k + 3 * jnp.minimum(k, 1), src])
            v = mm(pout[...], jnp.concatenate(parts, axis=0)).astype(BF)
            out_ref[pl.ds(pl.multiple_of(c * span + g * GROUP_ROWS, GROUP_ROWS), GROUP_ROWS)] = v

    term_stage(0)
    for copy in local[1:3]:
        copy.wait()

    @pl.loop(0, chunks + 4)
    def _(step):
        @pl.when(step + 1 < chunks)
        def _():
            term_stage(step + 1)

        @pl.when(step < chunks)
        def _():
            first_stage(step)

        @pl.when(step == 1)
        def _():
            for copy in local[3:7]:
                copy.wait()
            settle(w2s.at[pl.ds(4, 4)], w_recv.at[0])
            settle(w2c.at[pl.ds(4, 4)], w_recv.at[1])
            settle(b2, w_recv.at[2])

        @pl.when((step >= 1) & (step <= chunks))
        def _():
            second_stage(step - 1)

        @pl.when((step >= 2) & (step <= chunks + 1))
        def _():
            switch_stage(step - 2)

        @pl.when(step == 3)
        def _():
            for copy in local[7:]:
                copy.wait()
            settle(wzs.at[pl.ds(1, 3)], w_recv.at[3])
            settle(wzc.at[pl.ds(1, 3)], w_recv.at[4])
            settle(bz.at[pl.ds(1, 3)], w_recv.at[5])

        @pl.when((step >= 3) & (step <= chunks + 2))
        def _():
            last_stage(step - 3)

        @pl.when(step >= 4)
        def _():
            output_stage(step - 4)

    settle(w2s.at[pl.ds(4, 4)], w_send.at[0])
    settle(w2c.at[pl.ds(4, 4)], w_send.at[1])
    settle(b2, w_send.at[2])
    settle(wzs.at[pl.ds(1, 3)], w_send.at[3])
    settle(wzc.at[pl.ds(1, 3)], w_send.at[4])
    settle(bz.at[pl.ds(1, 3)], w_send.at[5])

    @pl.loop(0, chunks)
    def _(c):
        settle(ts.at[c], t_send)
        settle(hb.at[c, pl.ds(8, 4)], h_send)
        settle(ab.at[c, pl.ds(16, 15)], a_send)
        settle(zb.at[c, :, pl.ds(4, 3)], z_send)
        settle(rb.at[c, :, pl.ds(4, 3)], r_send)


def per_device(source_field, self_weight, cross_weight, level_bias, switch_weight, switch_bias):
    shots, blocks, width = source_field.shape
    chunks = CHUNKS
    rows = shots // chunks
    anywhere = pl.BlockSpec(memory_space=pl.ANY)
    vmem = pl.BlockSpec(memory_space=pltpu.VMEM)
    dma = pltpu.SemaphoreType.DMA
    square = (width, width)
    out = pl.pallas_call(
        functools.partial(kernel, chunks, rows),
        out_shape=pltpu.VMEM((shots * blocks, width), BF),
        in_specs=[anywhere] * 6,
        out_specs=vmem,
        scratch_shapes=[
            pltpu.VMEM((chunks, rows * 8, width), BF),
            pltpu.VMEM((chunks, 8, rows, width), BF),
            pltpu.VMEM((chunks, 8, rows, width), BF),
            pltpu.VMEM((chunks, 8, rows, width), BF),
            pltpu.VMEM((chunks, 12, rows, width), BF),
            pltpu.VMEM((8, rows, width), BF),
            pltpu.VMEM((chunks, 31, rows, 128), BF),
            pltpu.VMEM((8, rows, width), BF),
            pltpu.VMEM((chunks, 2, 7, rows, width), BF),
            pltpu.VMEM((2, 4, rows, width), BF),
            pltpu.VMEM((chunks, 2, 7, rows, width), BF),
            pltpu.VMEM((8,) + square, BF),
            pltpu.VMEM((8,) + square, BF),
            pltpu.VMEM((8,) + square, BF),
            pltpu.VMEM((8,) + square, BF),
            pltpu.VMEM((8,) + square, BF),
            pltpu.VMEM((4, 2, 2) + square, BF),
            pltpu.VMEM((4, 2, 2) + square, BF),
            pltpu.VMEM((4, 8, width), F32),
            pltpu.VMEM((8, width), F32),
            pltpu.VMEM((8, width), F32),
            pltpu.VMEM((4, 2, 8, width), F32),
            pltpu.VMEM((GROUP_ROWS, GROUP_ROWS), BF),
            pltpu.VMEM((GROUP_ROWS, GROUP_ROWS), BF),
            dma((chunks,)), dma((10,)), dma((6,)), dma((6,)),
            dma, dma((chunks,)),
            dma, dma((chunks,)),
            dma, dma((chunks,)),
            dma, dma((chunks, 2)),
            dma, dma((chunks,)),
        ],
        compiler_params=pltpu.CompilerParams(
            collective_id=0, has_side_effects=True, vmem_limit_bytes=56 * 1024 * 1024
        ),
        name="butterfly",
    )(
        source_field.reshape(shots * blocks, width),
        self_weight, cross_weight, level_bias, switch_weight, switch_bias,
    )
    return out.reshape(shots, blocks, width)


def solution(mesh):
    placed = (
        P(None, ("src", "tgt"), None),
        P(None, ("src", "tgt"), None, None),
        P(None, ("src", "tgt"), None, None),
        P(None, ("src", "tgt"), None),
        P(("src", "tgt"), None, None),
        P(("src", "tgt"), None),
    )
    return jax.shard_map(
        per_device,
        mesh=mesh,
        in_specs=placed,
        out_specs=P(None, ("src", "tgt"), None),
        check_vma=False,
    )
```

```python
import functools

import jax
import jax.numpy as jnp
from jax import lax
from jax.experimental import pallas as pl
from jax.experimental.pallas import tpu as pltpu
from jax.sharding import PartitionSpec as P

MESH = pl.DeviceIdType.MESH
BF = jnp.bfloat16
F32 = jnp.float32
CHUNKS = 8
GROUP_ROWS = 256


def mm(a, b):
    return jnp.dot(a, b, preferred_element_type=F32)


def finish(v):
    return jnp.maximum(v, 0.0).astype(BF)


def quarters(tiles):
    return [
        jnp.concatenate([tile[:, 32 * j : 32 * j + 32] for tile in tiles], axis=1)
        for j in range(4)
    ]


def ring(v):
    return lax.rem(v + 8, 4)


def kernel(
    chunks, rows,
    x_hbm, sw_hbm, cw_hbm, lb_hbm, gw_hbm, gb_hbm, out_ref,
    xio, xh, ts, tr, hb, h2, ab, mx, zb, h3, rb,
    w1s, w1c, w2s, w2c, ws, wzs, wzc, lb, gb, b2, bz, pin, pout,
    xin_sem, local_sem, w_send, w_recv,
    t_send, t_recv, h_send, h_recv, a_send, a_recv, z_send, z_recv, r_send, r_recv,
):
    s, t = lax.axis_index("src"), lax.axis_index("tgt")
    core, z, x_lo = lax.rem(s, 2), lax.rem(s // 2, 4), s // 8
    x_hi, y = lax.rem(t, 2), t // 2
    x = x_hi * 2 + x_lo

    def dev(x_, y_, z_, core_):
        return ((lax.rem(x_, 2) * 4 + z_) * 2 + core_, y_ * 2 + x_ // 2)

    core_peer = dev(x, y, z, 1 - core)
    x_peer = dev(x_hi * 2 + 1 - x_lo, y, z, core)

    def z_peer(k):
        return dev(x, y, ring(z + k), core)

    def xy_peer(w):
        return dev(ring(x + w // 4), ring(y + lax.rem(w, 4)), z, core)

    span = rows * 8

    def x_copy(c):
        part = pl.ds(pl.multiple_of(c * span, span), span)
        return pltpu.make_async_copy(x_hbm.at[part], xio.at[c], xin_sem.at[c])

    local = [
        pltpu.make_async_copy(cw_hbm.at[0], w1c, local_sem.at[0]),
        pltpu.make_async_copy(sw_hbm.at[0], w1s, local_sem.at[1]),
        pltpu.make_async_copy(lb_hbm, lb, local_sem.at[7]),
        pltpu.make_async_copy(sw_hbm.at[1, pl.ds(4 * x_lo, 4)], w2s.at[pl.ds(0, 4)], local_sem.at[2]),
        pltpu.make_async_copy(cw_hbm.at[1, pl.ds(4 * x_lo, 4)], w2c.at[pl.ds(0, 4)], local_sem.at[3]),
        pltpu.make_async_copy(gw_hbm, ws, local_sem.at[4]),
        pltpu.make_async_copy(gb_hbm, gb, local_sem.at[8]),
        pltpu.make_async_copy(sw_hbm.at[pl.ds(2, 2), pl.ds(2 * z, 2)], wzs.at[0], local_sem.at[5]),
        pltpu.make_async_copy(cw_hbm.at[pl.ds(2, 2), pl.ds(2 * z, 2)], wzc.at[0], local_sem.at[6]),
        pltpu.make_async_copy(lb_hbm.at[pl.ds(2, 2)], bz.at[0], local_sem.at[9]),
    ]
    x_copy(0).start()
    for copy in local[:3]:
        copy.start()

    barrier = pltpu.get_barrier_semaphore()

    def greet(device):
        pl.semaphore_signal(barrier, inc=1, device_id=device, device_id_type=MESH)

    greet(core_peer)
    for w in range(1, 16):
        greet(xy_peer(w))
    for k in range(1, 4):
        greet(z_peer(k))

    row = lax.broadcasted_iota(jnp.int32, (GROUP_ROWS, GROUP_ROWS), 0)
    col = lax.broadcasted_iota(jnp.int32, (GROUP_ROWS, GROUP_ROWS), 1)
    pin[...] = jnp.where(col == lax.rem(row, 32) * 8 + row // 32, 1.0, 0.0).astype(BF)
    pout[...] = jnp.where(row == lax.rem(col, 32) * 8 + col // 32, 1.0, 0.0).astype(BF)

    pl.semaphore_wait(barrier, 19)

    def send(src, dst, send_sem, recv_sem, device):
        pltpu.make_async_remote_copy(
            src_ref=src, dst_ref=dst, send_sem=send_sem, recv_sem=recv_sem,
            device_id=device, device_id_type=MESH,
        ).start()

    def settle(ref, sem):
        pltpu.make_async_copy(ref, ref, sem).wait()

    away = pl.ds(4 * (1 - x_lo), 4)
    send(sw_hbm.at[1, away], w2s.at[pl.ds(4, 4)], w_send.at[0], w_recv.at[0], x_peer)
    send(cw_hbm.at[1, away], w2c.at[pl.ds(4, 4)], w_send.at[1], w_recv.at[1], x_peer)
    send(lb_hbm.at[1], b2, w_send.at[2], w_recv.at[2], x_peer)
    for k in (2, 1, 3):
        blocks = pl.ds(2 * ring(z + k), 2)
        send(sw_hbm.at[pl.ds(2, 2), blocks], wzs.at[k], w_send.at[3], w_recv.at[3], z_peer(k))
        send(cw_hbm.at[pl.ds(2, 2), blocks], wzc.at[k], w_send.at[4], w_recv.at[4], z_peer(k))
        send(lb_hbm.at[pl.ds(2, 2)], bz.at[k], w_send.at[5], w_recv.at[5], z_peer(k))
    for copy in local[3:]:
        copy.start()

    @pl.loop(1, chunks)
    def _(c):
        x_copy(c).start()

    local[0].wait()

    def term_stage(c):
        x_copy(c).wait()

        for g in range(rows // 32):
            part = pl.ds(pl.multiple_of(g * GROUP_ROWS, GROUP_ROWS), GROUP_ROWS)
            v = mm(pin[...], xio[c, part]).astype(BF)
            dst = pl.ds(pl.multiple_of(g * 32, 32), 32)
            for l in range(8):
                xh[c, l, dst] = v[32 * l : 32 * l + 32]

        for l in range(8):
            ts[c, l] = mm(xh[c, l], w1c[l]).astype(BF)

        send(ts.at[c], tr.at[c], t_send, t_recv.at[c], core_peer)

    def first_stage(c):
        settle(tr.at[c], t_recv.at[c])
        for side in range(2):
            for m in range(4):
                l = 4 * (1 - x_lo if side == 0 else x_lo) + m
                v = mm(xh[c, l], w1s[l]) + tr[c, l].astype(F32) + lb[0, pl.ds(l, 1)]
                hb[c, l] = finish(v)
            if side == 0:
                send(hb.at[c, away], hb.at[c, pl.ds(8, 4)], h_send, h_recv.at[c], x_peer)

    def second_stage(c):
        settle(hb.at[c, pl.ds(8, 4)], h_recv.at[c])

        for m in range(4):
            l = 4 * x_lo + m
            mine, other = hb[c, l], hb[c, 8 + m]
            h2[m] = finish(mm(mine, w2s[m]) + mm(other, w2c[4 + m]) + lb[1, pl.ds(l, 1)])
            h2[4 + m] = finish(mm(other, w2s[4 + m]) + mm(mine, w2c[m]) + b2[pl.ds(l, 1)])

        for side in range(2):
            x_to = x_lo + side - 2 * x_lo * side
            for half in range(2):
                lanes = pl.ds(128 * half, 128)
                out = quarters([h2[4 * side + m, :, lanes] for m in range(4)])
                for u in range(4):
                    j = 4 * half + u
                    r = ring((j % 2) * 2 + x_to - x)
                    q = ring(j // 2 - y)
                    ab[c, r * 4 + q] = out[u]
        for w in range(1, 16):
            send(ab.at[c, w], ab.at[c, 15 + w], a_send, a_recv.at[c], xy_peer(w))

    def switch_stage(c):
        settle(ab.at[c, pl.ds(16, 15)], a_recv.at[c])

        for e in range(2):
            for half in range(2):
                tiles = []
                for u in range(4):
                    g = 4 * half + u
                    r = ring(x - ((g % 2) * 2 + e))
                    q = ring(y - g // 2)
                    w = r * 4 + q
                    tiles.append(ab[c, w + 15 * jnp.minimum(w, 1)])
                out = quarters(tiles)
                for m in range(4):
                    mx[4 * e + m, :, pl.ds(128 * half, 128)] = out[m]

        for n in range(2):
            for k in (2, 1, 3, 0):
                l = 2 * ring(z + k) + n
                zb[c, n, k] = finish(mm(mx[l], ws[l]) + gb[pl.ds(l, 1)])
            for k in (2, 1, 3):
                send(zb.at[c, n, k], zb.at[c, n, 3 + k], z_send, z_recv.at[c, n], z_peer(k))

    def last_stage(c):
        for n in range(2):
            settle(zb.at[c, n, pl.ds(4, 3)], z_recv.at[c, n])
            bias = pl.ds(2 * z + n, 1)
            held = [zb[c, n, k + 3 if k else 0] for k in range(4)]
            for k in range(4):
                k2 = (k + 2) % 4
                v = mm(held[k], wzs[k, 0, n]) + mm(held[k2], wzc[k2, 0, n]) + bz[k, 0, bias]
                h3[n, k] = finish(v)
            for k in (2, 1, 3, 0):
                home = ring(z - k)
                k1 = ring(z - (home + 1 - 2 * lax.rem(home, 2)))
                v = mm(h3[n, k], wzs[k, 1, n]) + mm(h3[n, k1], wzc[k1, 1, n]) + bz[k, 1, bias]
                rb[c, n, k] = finish(v)
            for k in (2, 1, 3):
                send(rb.at[c, n, k], rb.at[c, n, 3 + k], r_send, r_recv.at[c], z_peer(4 - k))

    def output_stage(c):
        settle(rb.at[c, :, pl.ds(4, 3)], r_recv.at[c])

        for g in range(rows // 32):
            src = pl.ds(pl.multiple_of(g * 32, 32), 32)
            parts = []
            for l in range(8):
                k = ring(l // 2 - z)
                parts.append(rb[c, l % 2, k + 3 * jnp.minimum(k, 1), src])
            v = mm(pout[...], jnp.concatenate(parts, axis=0)).astype(BF)
            out_ref[pl.ds(pl.multiple_of(c * span + g * GROUP_ROWS, GROUP_ROWS), GROUP_ROWS)] = v

    term_stage(0)
    for copy in local[1:3]:
        copy.wait()

    @pl.loop(0, chunks + 4)
    def _(step):
        @pl.when(step + 1 < chunks)
        def _():
            term_stage(step + 1)

        @pl.when(step < chunks)
        def _():
            first_stage(step)

        @pl.when(step == 1)
        def _():
            for copy in local[3:7]:
                copy.wait()
            settle(w2s.at[pl.ds(4, 4)], w_recv.at[0])
            settle(w2c.at[pl.ds(4, 4)], w_recv.at[1])
            settle(b2, w_recv.at[2])

        @pl.when((step >= 1) & (step <= chunks))
        def _():
            second_stage(step - 1)

        @pl.when((step >= 2) & (step <= chunks + 1))
        def _():
            switch_stage(step - 2)

        @pl.when(step == 3)
        def _():
            for copy in local[7:]:
                copy.wait()
            settle(wzs.at[pl.ds(1, 3)], w_recv.at[3])
            settle(wzc.at[pl.ds(1, 3)], w_recv.at[4])
            settle(bz.at[pl.ds(1, 3)], w_recv.at[5])

        @pl.when((step >= 3) & (step <= chunks + 2))
        def _():
            last_stage(step - 3)

        @pl.when(step >= 4)
        def _():
            output_stage(step - 4)

    settle(w2s.at[pl.ds(4, 4)], w_send.at[0])
    settle(w2c.at[pl.ds(4, 4)], w_send.at[1])
    settle(b2, w_send.at[2])
    settle(wzs.at[pl.ds(1, 3)], w_send.at[3])
    settle(wzc.at[pl.ds(1, 3)], w_send.at[4])
    settle(bz.at[pl.ds(1, 3)], w_send.at[5])

    @pl.loop(0, chunks)
    def _(c):
        settle(ts.at[c], t_send)
        settle(hb.at[c, pl.ds(8, 4)], h_send)
        settle(ab.at[c, pl.ds(16, 15)], a_send)
        settle(zb.at[c, :, pl.ds(4, 3)], z_send)
        settle(rb.at[c, :, pl.ds(4, 3)], r_send)


def per_device(source_field, self_weight, cross_weight, level_bias, switch_weight, switch_bias):
    shots, blocks, width = source_field.shape
    chunks = CHUNKS
    rows = shots // chunks
    anywhere = pl.BlockSpec(memory_space=pl.ANY)
    vmem = pl.BlockSpec(memory_space=pltpu.VMEM)
    dma = pltpu.SemaphoreType.DMA
    square = (width, width)
    out = pl.pallas_call(
        functools.partial(kernel, chunks, rows),
        out_shape=pltpu.VMEM((shots * blocks, width), BF),
        in_specs=[anywhere] * 6,
        out_specs=vmem,
        scratch_shapes=[
            pltpu.VMEM((chunks, rows * 8, width), BF),
            pltpu.VMEM((chunks, 8, rows, width), BF),
            pltpu.VMEM((chunks, 8, rows, width), BF),
            pltpu.VMEM((chunks, 8, rows, width), BF),
            pltpu.VMEM((chunks, 12, rows, width), BF),
            pltpu.VMEM((8, rows, width), BF),
            pltpu.VMEM((chunks, 31, rows, 128), BF),
            pltpu.VMEM((8, rows, width), BF),
            pltpu.VMEM((chunks, 2, 7, rows, width), BF),
            pltpu.VMEM((2, 4, rows, width), BF),
            pltpu.VMEM((chunks, 2, 7, rows, width), BF),
            pltpu.VMEM((8,) + square, BF),
            pltpu.VMEM((8,) + square, BF),
            pltpu.VMEM((8,) + square, BF),
            pltpu.VMEM((8,) + square, BF),
            pltpu.VMEM((8,) + square, BF),
            pltpu.VMEM((4, 2, 2) + square, BF),
            pltpu.VMEM((4, 2, 2) + square, BF),
            pltpu.VMEM((4, 8, width), F32),
            pltpu.VMEM((8, width), F32),
            pltpu.VMEM((8, width), F32),
            pltpu.VMEM((4, 2, 8, width), F32),
            pltpu.VMEM((GROUP_ROWS, GROUP_ROWS), BF),
            pltpu.VMEM((GROUP_ROWS, GROUP_ROWS), BF),
            dma((chunks,)), dma((10,)), dma((6,)), dma((6,)),
            dma, dma((chunks,)),
            dma, dma((chunks,)),
            dma, dma((chunks,)),
            dma, dma((chunks, 2)),
            dma, dma((chunks,)),
        ],
        compiler_params=pltpu.CompilerParams(
            collective_id=0, has_side_effects=True, vmem_limit_bytes=56 * 1024 * 1024
        ),
        name="butterfly",
    )(
        source_field.reshape(shots * blocks, width),
        self_weight, cross_weight, level_bias, switch_weight, switch_bias,
    )
    return out.reshape(shots, blocks, width)


def solution(mesh):
    placed = (
        P(None, ("src", "tgt"), None),
        P(None, ("src", "tgt"), None, None),
        P(None, ("src", "tgt"), None, None),
        P(None, ("src", "tgt"), None),
        P(("src", "tgt"), None, None),
        P(("src", "tgt"), None),
    )
    return jax.shard_map(
        per_device,
        mesh=mesh,
        in_specs=placed,
        out_specs=P(None, ("src", "tgt"), None),
        check_vma=False,
    )
```
